32 devices in a mesh: grp: 2 (over y), row: 4 (over z), col: 2 (over x), slc: 2 (over core).
Axes of the slice: x: 2, y: 2, z: 4, core: 2. Of those that a mesh axis runs over, the one named last changes fastest.
Arguments:
- objects: bfloat16 [2, 2, 3072, 768], P(None, None, ('grp', 'row'), 'col'), parts along dimension 2, may hold values from -1 to 1
- probes: bfloat16 [4, 2, 256, 256], P(('grp', 'slc')), parts along dimension 0, may hold values from -3 to 3
- weights: float32 [256, 256], replicated, may hold values from 0.1 to 1
- counts: int32 [8, 2], P(('grp', 'row'), 'col'), parts along dimension 0, may hold values from 1 to 2, as said below
- offsets: int32 [8, 2, 2, 2], P(('grp', 'row'), 'col'), parts along dimension 0, may hold values from 0 to 383, as said below
- intensities: bfloat16 [8, 2, 2, 256, 256], P(('grp', 'row'), 'col'), parts along dimension 0, may hold values from 0.049804688 to 2
Outputs:
- gradient: float32 [2, 2, 3072, 768], P('slc', None, ('grp', 'row'), 'col'), parts along dimension 2
The draws below stay inside these ranges and needn't reach their ends.
There are 2 independent parts, one for each index of `grp`. The reference program is written for one: setup_inputs(seed, part) draws one part's arguments, and reference() takes and returns one part's arrays. A program takes and returns all parts, laid end to end along the dimension named above; an argument that names none is the same for every part. Nothing has to cross between parts.
Inputs may be any that keep to these rules, and one draw needn't show every extreme that they name: `counts`: some tile has exactly 2 positions. `offsets`: every window of a live position lies inside the object; entries of slots at or after a tile's count are ignored.
All inputs are finite; a program needn't handle non-finite values.
Results may differ from the reference program's by a relative error of at most 0.019.
Values may be sent and summed in bfloat16 or wider, within the bound.
A program may use at most 64 MiB of HBM per device.

```python
import math
import jax
import jax.numpy as jnp
from jax import lax

WIN = 256
TILE = 384
SLOTS = 2
SLICES = 2
MODES = 2
NY = 1536
NX = 768
N_ROW = 4
N_COL = 2


def draw_counts(key, part):
    earlier_key = jax.random.fold_in(key, 11)
    another_key = jax.random.fold_in(key, 12)
    picked_key = jax.random.fold_in(key, 13)
    earlier = jax.random.randint(earlier_key, (N_ROW, N_COL), 1, SLOTS + 1)
    another = jax.random.randint(another_key, (N_ROW, N_COL), 1, SLOTS + 1)
    lowest = jnp.minimum(earlier, another)
    picked = jax.random.randint(picked_key, (), 0, N_ROW * N_COL)
    places = jnp.arange(N_ROW * N_COL, dtype=jnp.int32).reshape(N_ROW, N_COL)
    return jnp.where(places == picked, SLOTS, lowest).astype(jnp.int32)


def draw_offsets(key, part):
    tile_rows = jnp.arange(N_ROW, dtype=jnp.int32)[:, None, None, None]
    tile_cols = jnp.arange(N_COL, dtype=jnp.int32)[None, :, None, None]
    component = jnp.arange(2, dtype=jnp.int32)[None, None, None, :]
    last_row = (tile_rows == N_ROW - 1) & (component == 0)
    last_col = (tile_cols == N_COL - 1) & (component == 1)
    ceiling = jnp.where(last_row | last_col, TILE - WIN + 1, TILE)
    ceiling = jnp.broadcast_to(ceiling, (N_ROW, N_COL, SLOTS, 2))
    return jax.random.randint(jax.random.fold_in(key, 21), (N_ROW, N_COL, SLOTS, 2), 0, ceiling).astype(jnp.int32)


def steps_of(key, shape, shards, least, top_value):
    def one(position, shards_of):
        heights = jax.random.uniform(jax.random.fold_in(jax.random.fold_in(key, 6), position), (shards_of,), jnp.float32, least / len(shards), top_value / len(shards))
        return jnp.repeat(jnp.exp(heights), shape[position] // shards_of).reshape((-1,) + (1,) * (len(shape) - position - 1))

    gain = one(*shards[0])
    for cut in shards[1:]:
        gain = gain * one(*cut)
    return gain


def noise(rng, shape, deviation, most, pieces=(), held_as=jnp.bfloat16):
    loudness = steps_of(rng, shape, pieces, -0.22, 0.18) if pieces else 1.0
    entries = jax.random.normal(rng, shape, jnp.float32) * deviation * loudness
    return jnp.minimum(jnp.maximum(entries, -most), most).astype(held_as)


def setup_inputs(seed: int = 0, part: int = 0) -> dict:
    key_list = jax.random.split(jax.random.key(seed), 7)
    part_splits = jax.random.split(jax.random.fold_in(key_list[6], part), 7)
    return {
        "objects": jnp.clip(jax.random.uniform(part_splits[0], (SLICES, 2, NY, NX), jnp.float32, -1.0, 1.0) * steps_of(part_splits[0], (SLICES, 2, NY, NX), ((2, 4), (3, 2)), -0.4, 0.0), -1.0, 1.0).astype(jnp.bfloat16),
        "probes": noise(part_splits[1], (MODES, 2, WIN, WIN), 0.5, 3.0, ((0, 2),)),
        "weights": jnp.clip(jnp.exp(jax.random.uniform(key_list[2], (WIN, WIN), jnp.float32, math.log(0.1), math.log(1.0))), 0.1, 1.0),
        "counts": draw_counts(jax.random.fold_in(jax.random.fold_in(key_list[6], part), 71), part),
        "offsets": draw_offsets(jax.random.fold_in(jax.random.fold_in(key_list[6], part), 71), part),
        "intensities": jnp.clip(jnp.exp(math.log(2.0) - 3.6927934 * jax.random.uniform(part_splits[5], (N_ROW, N_COL, SLOTS, WIN, WIN), jnp.float32) ** steps_of(part_splits[5], (N_ROW, N_COL, SLOTS, WIN, WIN), ((0, 4), (1, 2)), -0.2, 0.2)), 0.049804688, 2.0).astype(jnp.bfloat16),
    }


fresnel = 0.5

def dft_tables(extent):
    counter = jnp.arange(extent, dtype=jnp.int32)
    product = counter[:, None] * counter[None, :] % extent
    angles = 2.0 * jnp.pi / extent * product.astype(jnp.float32)
    norm_scale = 1.0 / jnp.sqrt(jnp.asarray(extent, jnp.float32))
    table_re = (jnp.cos(angles) * norm_scale).astype(jnp.bfloat16)
    table_im = (-jnp.sin(angles) * norm_scale).astype(jnp.bfloat16)
    return (table_re, table_im)

def chirp_factor(extent):
    counter = jnp.arange(extent, dtype=jnp.int32)
    signed_freq = (counter + extent // 2) % extent - extent // 2
    squares = signed_freq[:, None] * signed_freq[:, None] + signed_freq[None, :] * signed_freq[None, :]
    angles = -jnp.pi * fresnel / extent * squares.astype(jnp.float32)
    return (jnp.cos(angles), jnp.sin(angles))

def transform(real, imag, table_re, table_im):
    real_half = real.astype(jnp.bfloat16)
    imag_half = imag.astype(jnp.bfloat16)
    mid_re = jnp.dot(table_re, real_half, preferred_element_type=jnp.float32) - jnp.dot(table_im, imag_half, preferred_element_type=jnp.float32)
    mid_im = jnp.dot(table_re, imag_half, preferred_element_type=jnp.float32) + jnp.dot(table_im, real_half, preferred_element_type=jnp.float32)
    mid_re = mid_re.astype(jnp.bfloat16)
    mid_im = mid_im.astype(jnp.bfloat16)
    out_re = jnp.dot(mid_re, table_re, preferred_element_type=jnp.float32) - jnp.dot(mid_im, table_im, preferred_element_type=jnp.float32)
    out_im = jnp.dot(mid_re, table_im, preferred_element_type=jnp.float32) + jnp.dot(mid_im, table_re, preferred_element_type=jnp.float32)
    return (out_re, out_im)

def complex_mul(left_re, left_im, right_re, right_im):
    return (left_re * right_re - left_im * right_im, left_re * right_im + left_im * right_re)

def conj_mul(left_re, left_im, right_re, right_im):
    return (left_re * right_re + left_im * right_im, left_re * right_im - left_im * right_re)

def forward_mode(probe_re, probe_im, window, tables, chirps):
    table_re, table_im, inverse_im = tables
    chirp_re, chirp_im = chirps
    first_re = window[0, 0].astype(jnp.float32)
    first_im = window[0, 1].astype(jnp.float32)
    second_re = window[1, 0].astype(jnp.float32)
    second_im = window[1, 1].astype(jnp.float32)
    psi_re, psi_im = complex_mul(probe_re, probe_im, first_re, first_im)
    spec_re, spec_im = transform(psi_re, psi_im, table_re, table_im)
    spec_re, spec_im = complex_mul(chirp_re, chirp_im, spec_re, spec_im)
    prop_re, prop_im = transform(spec_re, spec_im, table_re, inverse_im)
    exit_re, exit_im = complex_mul(prop_re, prop_im, second_re, second_im)
    far_re, far_im = transform(exit_re, exit_im, table_re, table_im)
    return (prop_re, prop_im, far_re, far_im)

def backward_mode(probe_re, probe_im, window, prop_re, prop_im, far_re, far_im, residual, tables, chirps):
    table_re, table_im, inverse_im = tables
    chirp_re, chirp_im = chirps
    second_re = window[1, 0].astype(jnp.float32)
    second_im = window[1, 1].astype(jnp.float32)
    back_re, back_im = transform(residual * far_re, residual * far_im, table_re, inverse_im)
    grad_two_re, grad_two_im = conj_mul(prop_re, prop_im, back_re, back_im)
    gprop_re, gprop_im = conj_mul(second_re, second_im, back_re, back_im)
    gspec_re, gspec_im = transform(gprop_re, gprop_im, table_re, table_im)
    gspec_re, gspec_im = conj_mul(chirp_re, chirp_im, gspec_re, gspec_im)
    gpsi_re, gpsi_im = transform(gspec_re, gspec_im, table_re, inverse_im)
    grad_one_re, grad_one_im = conj_mul(probe_re, probe_im, gpsi_re, gpsi_im)
    return jnp.stack([jnp.stack([grad_one_re, grad_one_im]), jnp.stack([grad_two_re, grad_two_im])])

def reference(objects, probes, weights, counts, offsets, intensities):
    slices = objects.shape[0]
    height = objects.shape[2]
    breadth = objects.shape[3]
    extent = probes.shape[2]
    tile_size = height // N_ROW
    table_re, table_im = dft_tables(extent)
    tables = (table_re, table_im, -table_im)
    chirps = chirp_factor(extent)
    padded = jnp.pad(objects, ((0, 0), (0, 0), (0, extent), (0, extent)))
    slot_total = N_ROW * N_COL * SLOTS
    serial = jnp.arange(slot_total, dtype=jnp.int32)
    tile_row = serial // (N_COL * SLOTS)
    tile_col = serial // SLOTS % N_COL
    slot_of = serial % SLOTS
    flat_offsets = offsets.reshape(slot_total, 2).astype(jnp.int32)
    top_rows = (tile_row * tile_size + flat_offsets[:, 0]).astype(jnp.int32)
    left_cols = (tile_col * tile_size + flat_offsets[:, 1]).astype(jnp.int32)
    alive_mask = slot_of < counts.reshape(-1)[serial // SLOTS]
    measured = intensities.reshape(slot_total, extent, extent)

    def slot_term(window, data_slot):
        forwards = []
        intensity = jnp.zeros((extent, extent), jnp.float32)
        for mode_id in range(probes.shape[0]):
            probe_re = probes[mode_id, 0].astype(jnp.float32)
            probe_im = probes[mode_id, 1].astype(jnp.float32)
            result = forward_mode(probe_re, probe_im, window, tables, chirps)
            forwards.append(result)
            intensity = intensity + result[2] * result[2] + result[3] * result[3]
        residual = 2.0 * weights * (intensity - data_slot.astype(jnp.float32))
        contrib = jnp.zeros((slices, 2, extent, extent), jnp.float32)
        for mode_id in range(probes.shape[0]):
            probe_re = probes[mode_id, 0].astype(jnp.float32)
            probe_im = probes[mode_id, 1].astype(jnp.float32)
            prop_re, prop_im, far_re, far_im = forwards[mode_id]
            contrib = contrib + backward_mode(probe_re, probe_im, window, prop_re, prop_im, far_re, far_im, residual, tables, chirps)
        return contrib

    def accumulate(gradient, inputs):
        top, left, alive, data_slot = inputs
        anchor = jnp.int32(0)
        window = lax.dynamic_slice(padded, (anchor, anchor, top, left), (slices, 2, extent, extent))
        contrib = lax.cond(alive, slot_term, lambda window_in, data_in: jnp.zeros((slices, 2, extent, extent), jnp.float32), window, data_slot)
        previous = lax.dynamic_slice(gradient, (anchor, anchor, top, left), (slices, 2, extent, extent))
        gradient = lax.dynamic_update_slice(gradient, previous + contrib, (anchor, anchor, top, left))
        return (gradient, None)
    initial = jnp.zeros((slices, 2, height + extent, breadth + extent), jnp.float32)
    gradient, _ = lax.scan(accumulate, initial, (top_rows, left_cols, alive_mask, measured))
    return gradient[:, :, :height, :breadth]
```

```python
import functools

import jax
import jax.numpy as jnp
import ml_dtypes
import numpy as np
from jax import lax
from jax.experimental import pallas as pl
from jax.experimental.pallas import tpu as pltpu
from jax.sharding import PartitionSpec as P

MESH = pl.DeviceIdType.MESH
fresnel = 0.5
f32 = jnp.float32
bf16 = jnp.bfloat16


def dft_tables(extent):
    counter = np.arange(extent, dtype=np.int64)
    product = counter[:, None] * counter[None, :] % extent
    angles = np.float32(2.0 * np.pi / extent) * product.astype(np.float32)
    norm_scale = np.float32(1.0 / np.sqrt(extent))
    real = (np.cos(angles) * norm_scale).astype(ml_dtypes.bfloat16)
    imag = (-np.sin(angles) * norm_scale).astype(ml_dtypes.bfloat16)
    plus = np.block([[real, -imag], [imag, real]])
    minus = np.block([[real, imag], [-imag, real]])
    return np.stack([plus, minus]).astype(ml_dtypes.bfloat16)


def chirp_factor(extent):
    counter = np.arange(extent, dtype=np.int64)
    signed = (counter + extent // 2) % extent - extent // 2
    squares = signed[:, None] ** 2 + signed[None, :] ** 2
    angles = np.float32(-np.pi * fresnel / extent) * squares.astype(np.float32)
    return np.stack([np.cos(angles), np.sin(angles)]).astype(np.float32)


def cmul(a, b):
    return (a[0] * b[0] - a[1] * b[1], a[0] * b[1] + a[1] * b[0])


def conj_mul(a, b):
    return (a[0] * b[0] + a[1] * b[1], a[0] * b[1] - a[1] * b[0])


def kernel(
    shape, off_ref, cnt_ref, obj, probes, weights, intens, tables, chirps, out_ref,
    ext1, ext2, prb, wts, inten, tab, chp, gsend, gpart,
    hb, hr, hd, rb, rr, rd, lsem, fsend, frecv, relsend, relrecv, psem, gsem, hsend, hrecv,
):
    rows_n, cols_n, T, E = shape
    row, col, k = lax.axis_index("row"), lax.axis_index("col"), lax.axis_index("slc")
    other = 1 - k
    exts = (ext1, ext2)
    has_right, has_left = col < cols_n - 1, col > 0
    has_below, has_above = row < rows_n - 1, row > 0
    partner = {"slc": other}
    up, down = {"row": row - 1}, {"row": row + 1}
    left, right = {"col": col - 1}, {"col": col + 1}
    up_left = {"row": row - 1, "col": col - 1}
    down_right = {"row": row + 1, "col": col + 1}
    sides = (
        (has_right, right), (has_left, left), (has_below, down), (has_above, up),
        (has_right & has_below, down_right), (has_left & has_above, up_left),
    )

    local = [
        pltpu.make_async_copy(obj.at[0], ext1.at[:, 0:T, 0:T], lsem.at[0]),
        pltpu.make_async_copy(obj.at[1], ext2.at[:, 0:T, 0:T], lsem.at[1]),
        pltpu.make_async_copy(probes.at[0], prb.at[k], lsem.at[2]),
        pltpu.make_async_copy(weights, wts, lsem.at[3]),
        pltpu.make_async_copy(intens.at[0, 0, k], inten, lsem.at[4]),
        pltpu.make_async_copy(tables, tab, lsem.at[5]),
        pltpu.make_async_copy(chirps, chp, lsem.at[6]),
    ]
    for one in local:
        one.start()

    barrier = pltpu.get_barrier_semaphore()
    pl.semaphore_signal(barrier, inc=1, device_id=partner, device_id_type=MESH)
    for there, who in sides:
        @pl.when(there)
        def _(who=who):
            pl.semaphore_signal(barrier, inc=1, device_id=who, device_id_type=MESH)
    peers = 1
    for there, _ in sides:
        peers = peers + there.astype(jnp.int32)
    pl.semaphore_wait(barrier, peers)

    def remote(src, dst, ssem, rsem, who):
        return pltpu.make_async_remote_copy(
            src_ref=src, dst_ref=dst, send_sem=ssem, recv_sem=rsem,
            device_id=who, device_id_type=MESH,
        )

    def place(piece):
        return (
            (slice(0, T), slice(T, T + E)),
            (slice(T, T + E), slice(0, T)),
            (slice(T, T + E), slice(T, T + E)),
        )[piece]

    def source(piece):
        return (
            (slice(0, T), slice(0, E)),
            (slice(0, E), slice(0, T)),
            (slice(0, E), slice(0, E)),
        )[piece]

    sends = (has_left, has_above, has_left & has_above)
    takes = (has_right, has_below, has_right & has_below)
    targets = (left, up, up_left)

    def halo(s, piece):
        return remote(
            obj.at[(s, k) + source(piece)], exts[s].at[(k,) + place(piece)],
            fsend.at[s, piece], frecv.at[s, piece], targets[piece],
        )

    def relay(s, piece):
        region = exts[s].at[(k,) + place(piece)]
        return remote(region, region, relsend.at[s, piece], relrecv.at[s, piece], partner)

    for s in range(2):
        for piece in range(3):
            @pl.when(sends[piece])
            def _(s=s, piece=piece):
                halo(s, piece).start()

    probe_copy = remote(probes.at[0], prb.at[k], psem.at[0], psem.at[1], partner)
    probe_copy.start()

    def arrive(s):
        for piece in range(3):
            @pl.when(takes[piece])
            def _(piece=piece):
                halo(s, piece).wait_recv()
                relay(s, piece).start()
        for piece in range(3):
            @pl.when(takes[piece])
            def _(piece=piece):
                relay(s, piece).wait_recv()
            @pl.when(jnp.logical_not(takes[piece]))
            def _(piece=piece):
                at = (slice(None),) + place(piece)
                exts[s][at] = jnp.zeros_like(exts[s][at])
        local[s].wait()

    oy, ox = off_ref[0, 0, k, 0], off_ref[0, 0, k, 1]

    W = T + E

    def pick(shape_of, axis, low, wrap=False):
        here = lax.broadcasted_iota(jnp.int32, shape_of, axis)
        there = lax.broadcasted_iota(jnp.int32, shape_of, 1 - axis) + low
        if wrap:
            there = there & (E - 1)
        return jnp.where(here == there, 1.0, 0.0).astype(bf16)

    def window(s):
        by_row, by_col = pick((E, W), 1, oy), pick((W, E), 0, ox)
        result = []
        for c in range(2):
            strip = jnp.dot(by_row, exts[s][c], preferred_element_type=f32).astype(bf16)
            result.append(jnp.dot(strip, by_col, preferred_element_type=f32))
        return tuple(result)

    def transform(v, forward):
        lhs, rhs = (tab.at[0], tab.at[1]) if forward else (tab.at[1], tab.at[0])
        stacked = jnp.concatenate([v[0].astype(bf16), v[1].astype(bf16)], axis=0)
        mid = jnp.dot(lhs[...], stacked, preferred_element_type=f32).astype(bf16)
        wide = jnp.concatenate([mid[0:E], mid[E:]], axis=1)
        result = jnp.dot(wide, rhs[...], preferred_element_type=f32)
        return (result[:, 0:E], result[:, E:])

    modes = range(2)
    for one in (2, 5, 6):
        local[one].wait()
    probe_copy.wait()
    arrive(0)

    def probe(m):
        return (prb[m, 0].astype(f32), prb[m, 1].astype(f32))

    def chirp():
        return (chp[0], chp[1])

    first = window(0)
    props = []
    for m in modes:
        spec = transform(cmul(probe(m), first), True)
        props.append(transform(cmul(chirp(), spec), False))
    arrive(1)
    second = window(1)
    fars = [transform(cmul(props[m], second), True) for m in modes]
    local[3].wait()
    local[4].wait()
    intensity = sum(f[0] * f[0] + f[1] * f[1] for f in fars)
    residual = 2.0 * wts[...] * (intensity - inten[...].astype(f32))
    backs = [transform((residual * fars[m][0], residual * fars[m][1]), False) for m in modes]

    alive = jnp.zeros((E, E), jnp.int32) + k < cnt_ref[0, 0]
    turn_y, turn_x = pick((E, E), 0, oy, True), pick((E, E), 1, ox, True)

    def finish(s, parts):
        for c in range(2):
            total = jnp.where(alive, parts[0][c] + parts[1][c], 0.0).astype(bf16)
            turned = jnp.dot(turn_y, total, preferred_element_type=f32).astype(bf16)
            gsend[s, c] = jnp.dot(turned, turn_x, preferred_element_type=f32).astype(bf16)

    give = remote(gsend.at[other], gpart, gsem.at[0], gsem.at[1], partner)
    finish(1, [conj_mul(props[m], backs[m]) for m in modes])

    @pl.when(k == 0)
    def _():
        give.start()

    ones = []
    for m in modes:
        gspec = transform(conj_mul(second, backs[m]), True)
        gpsi = transform(conj_mul(chirp(), gspec), False)
        ones.append(conj_mul(probe(m), gpsi))
    finish(0, ones)

    @pl.when(k == 1)
    def _():
        give.start()

    def mask(axis, slot, start, size):
        shape_of = (size, E) if axis == 0 else (E, size)
        place_of = lax.broadcasted_iota(jnp.int32, shape_of, axis) + start
        low = off_ref[0, 0, slot, axis]
        return (place_of >= low) & (place_of < low + E)

    give.wait_recv()
    half = E // 2

    def block(c, y, x, h, w):
        y0, x0 = y % E, x % E
        total = None
        for slot, values in (
            (k, gsend[k, c, y0 : y0 + h, x0 : x0 + w].astype(f32)),
            (other, gpart[c, y0 : y0 + h, x0 : x0 + w].astype(f32)),
        ):
            ypos = lax.broadcasted_iota(jnp.int32, (h, w), 0) + y
            xpos = lax.broadcasted_iota(jnp.int32, (h, w), 1) + x
            low_y, low_x = off_ref[0, 0, slot, 0], off_ref[0, 0, slot, 1]
            inside = (
                (ypos >= low_y) & (ypos < low_y + E) & (xpos >= low_x) & (xpos < low_x + E)
            )
            term = jnp.where(inside, values, 0.0)
            total = term if total is None else total + term
        return total

    def spans(start, stop):
        result = []
        while start < stop:
            end = min(stop, (start // half + 1) * half)
            result.append((start, end - start))
            start = end
        return result

    inner, outer = spans(0, T), spans(T, T + E)

    def fill(dst, ys, xs, y_base, x_base, dtype):
        for c in range(2):
            for y, h in ys:
                for x, w in xs:
                    dst[c, y - y_base : y - y_base + h, x - x_base : x - x_base + w] = block(
                        c, y, x, h, w
                    ).astype(dtype)

    targets_out = (down_right, right, down)
    send_out = (has_right & has_below, has_right, has_below)
    take_out = (has_left & has_above, has_left, has_above)
    sources_out, lands_out = (hd, hr, hb), (rd, rr, rb)

    def push(i):
        return remote(sources_out[i], lands_out[i], hsend.at[i], hrecv.at[i], targets_out[i])

    for i, (ys, xs, yb, xb) in enumerate(
        ((outer, outer, T, T), (inner, outer, 0, T), (outer, inner, T, 0))
    ):
        @pl.when(send_out[i])
        def _(i=i, ys=ys, xs=xs, yb=yb, xb=xb):
            fill(sources_out[i], ys, xs, yb, xb, bf16)
            push(i).start()
    fill(out_ref.at[0], inner, inner, 0, 0, f32)

    areas = ((slice(0, E), slice(0, E)), (slice(0, T), slice(0, E)), (slice(0, E), slice(0, T)))
    for i in (1, 2, 0):
        @pl.when(take_out[i])
        def _(i=i):
            push(i).wait_recv()
            for c in range(2):
                at = (0, c) + areas[i]
                out_ref[at] = out_ref[at] + lands_out[i][c].astype(f32)

    for s in range(2):
        for piece in range(3):
            @pl.when(sends[piece])
            def _(s=s, piece=piece):
                halo(s, piece).wait_send()

            @pl.when(takes[piece])
            def _(s=s, piece=piece):
                relay(s, piece).wait_send()
    give.wait_send()
    for i in range(3):
        @pl.when(send_out[i])
        def _(i=i):
            push(i).wait_send()


def solution(mesh):
    rows_n, cols_n = mesh.shape["row"], mesh.shape["col"]

    def body(objects, probes, weights, counts, offsets, intensities):
        T, E = objects.shape[2], probes.shape[2]
        W = T + E
        any_space = pl.BlockSpec(memory_space=pl.ANY)
        smem = pl.BlockSpec(memory_space=pltpu.SMEM)
        dma = pltpu.SemaphoreType.DMA
        return pl.pallas_call(
            functools.partial(kernel, (rows_n, cols_n, T, E)),
            out_shape=jax.ShapeDtypeStruct((1, 2, T, T), f32),
            in_specs=[smem, smem] + [any_space] * 6,
            out_specs=pl.BlockSpec(memory_space=pltpu.VMEM),
            scratch_shapes=[
                pltpu.VMEM((2, W, W), bf16), pltpu.VMEM((2, W, W), bf16),
                pltpu.VMEM((2, 2, E, E), bf16), pltpu.VMEM((E, E), f32),
                pltpu.VMEM((E, E), bf16), pltpu.VMEM((2, 2 * E, 2 * E), bf16),
                pltpu.VMEM((2, E, E), f32),
                pltpu.VMEM((2, 2, E, E), bf16),
                pltpu.VMEM((2, E, E), bf16),
                pltpu.VMEM((2, E, T), bf16), pltpu.VMEM((2, T, E), bf16), pltpu.VMEM((2, E, E), bf16),
                pltpu.VMEM((2, E, T), bf16), pltpu.VMEM((2, T, E), bf16), pltpu.VMEM((2, E, E), bf16),
                dma((7,)), dma((2, 3)), dma((2, 3)), dma((2, 3)), dma((2, 3)),
                dma((2,)), dma((2,)), dma((3,)), dma((3,)),
            ],
            compiler_params=pltpu.CompilerParams(
                collective_id=0, has_side_effects=True, vmem_limit_bytes=48 * 1024 * 1024
            ),
            name="ptycho",
        )(
            offsets, counts, objects, probes, weights, intensities,
            jnp.asarray(dft_tables(E)), jnp.asarray(chirp_factor(E)),
        )

    in_specs = (
        P(None, None, ("grp", "row"), "col"),
        P(("grp", "slc"), None, None, None),
        P(),
        P(("grp", "row"), "col"),
        P(("grp", "row"), "col", None, None),
        P(("grp", "row"), "col", None, None, None),
    )
    out_specs = P("slc", None, ("grp", "row"), "col")
    return jax.shard_map(body, mesh=mesh, in_specs=in_specs, out_specs=out_specs, check_vma=False)
```

```python
import functools

import jax
import jax.numpy as jnp
import ml_dtypes
import numpy as np
from jax import lax
from jax.experimental import pallas as pl
from jax.experimental.pallas import tpu as pltpu
from jax.sharding import PartitionSpec as P

MESH = pl.DeviceIdType.MESH
fresnel = 0.5
f32 = jnp.float32
bf16 = jnp.bfloat16


def dft_tables(extent):
    counter = np.arange(extent, dtype=np.int64)
    product = counter[:, None] * counter[None, :] % extent
    angles = np.float32(2.0 * np.pi / extent) * product.astype(np.float32)
    norm_scale = np.float32(1.0 / np.sqrt(extent))
    real = (np.cos(angles) * norm_scale).astype(ml_dtypes.bfloat16)
    imag = (-np.sin(angles) * norm_scale).astype(ml_dtypes.bfloat16)
    plus = np.block([[real, -imag], [imag, real]])
    minus = np.block([[real, imag], [-imag, real]])
    return np.stack([plus, minus]).astype(ml_dtypes.bfloat16)


def chirp_factor(extent):
    counter = np.arange(extent, dtype=np.int64)
    signed = (counter + extent // 2) % extent - extent // 2
    squares = signed[:, None] ** 2 + signed[None, :] ** 2
    angles = np.float32(-np.pi * fresnel / extent) * squares.astype(np.float32)
    return np.stack([np.cos(angles), np.sin(angles)]).astype(np.float32)


def cmul(a, b):
    return (a[0] * b[0] - a[1] * b[1], a[0] * b[1] + a[1] * b[0])


def conj_mul(a, b):
    return (a[0] * b[0] + a[1] * b[1], a[0] * b[1] - a[1] * b[0])


def kernel(
    shape, off_ref, cnt_ref, obj, probes, weights, intens, tables, chirps, out_ref,
    ext1, ext2, prb, wts, inten, tab, chp, gsend, gpart,
    hb, hr, hd, rb, rr, rd, lsem, fsend, frecv, relsend, relrecv, psem, gsem, hsend, hrecv,
):
    rows_n, cols_n, T, E = shape
    row, col, k = lax.axis_index("row"), lax.axis_index("col"), lax.axis_index("slc")
    other = 1 - k
    exts = (ext1, ext2)
    has_right, has_left = col < cols_n - 1, col > 0
    has_below, has_above = row < rows_n - 1, row > 0
    partner = {"slc": other}
    up, down = {"row": row - 1}, {"row": row + 1}
    left, right = {"col": col - 1}, {"col": col + 1}
    sides = (
        (has_right, right), (has_left, left), (has_below, down), (has_above, up),
    )

    local = [
        pltpu.make_async_copy(obj.at[0], ext1.at[:, 0:T, 0:T], lsem.at[0]),
        pltpu.make_async_copy(obj.at[1], ext2.at[:, 0:T, 0:T], lsem.at[1]),
        pltpu.make_async_copy(probes.at[0], prb.at[k], lsem.at[2]),
        pltpu.make_async_copy(weights, wts, lsem.at[3]),
        pltpu.make_async_copy(intens.at[0, 0, k], inten, lsem.at[4]),
        pltpu.make_async_copy(tables, tab, lsem.at[5]),
        pltpu.make_async_copy(chirps, chp, lsem.at[6]),
    ]
    for one in local:
        one.start()

    barrier = pltpu.get_barrier_semaphore()
    pl.semaphore_signal(barrier, inc=1, device_id=partner, device_id_type=MESH)
    for there, who in sides:
        @pl.when(there)
        def _(who=who):
            pl.semaphore_signal(barrier, inc=1, device_id=who, device_id_type=MESH)
    peers = 1
    for there, _ in sides:
        peers = peers + there.astype(jnp.int32)
    pl.semaphore_wait(barrier, peers)

    def remote(src, dst, ssem, rsem, who):
        return pltpu.make_async_remote_copy(
            src_ref=src, dst_ref=dst, send_sem=ssem, recv_sem=rsem,
            device_id=who, device_id_type=MESH,
        )

    W = T + E
    near, rest, far = slice(0, E), slice(E, T), slice(T, W)
    places = ((near, far), (far, near), (rest, far), (far, rest), (far, far))
    sources = ((near, near), (near, near), (rest, near), (near, rest))
    sends = (has_left, has_above, has_left, has_above)
    takes = (has_right, has_below, has_right, has_below, has_right & has_below)
    targets = (left, up, left, up)
    turn = (has_above & has_right, has_left & has_below)

    def halo(s, piece):
        return remote(
            obj.at[(s, k) + sources[piece]], exts[s].at[(k,) + places[piece]],
            fsend.at[s, piece], frecv.at[s, piece], targets[piece],
        )

    def corner(s, core):
        return remote(
            exts[s].at[(core,) + places[core]], exts[s].at[(core,) + places[4]],
            fsend.at[s, 4], frecv.at[s, 4], targets[1 - core],
        )

    def relay(s, piece):
        region = exts[s].at[(k,) + places[piece]]
        return remote(region, region, relsend.at[s, piece], relrecv.at[s, piece], partner)

    def start(s):
        for piece in range(4):
            @pl.when(sends[piece])
            def _(piece=piece):
                halo(s, piece).start()

    def hand_over(s, piece):
        @pl.when(takes[piece])
        def _():
            if piece < 4:
                halo(s, piece).wait_recv()
            else:
                corner(s, 0).wait_recv()
            relay(s, piece).start()

    def early(s):
        for core in range(2):
            @pl.when(k == core)
            def _(core=core):
                hand_over(s, core)

                @pl.when(turn[core])
                def _():
                    corner(s, core).start()

    def arrive(s):
        for core in range(2):
            @pl.when(k == core)
            def _(core=core):
                hand_over(s, 1 - core)
        for piece in (2, 3, 4):
            hand_over(s, piece)
        for piece in range(5):
            @pl.when(takes[piece])
            def _(piece=piece):
                relay(s, piece).wait_recv()
        local[s].wait()

    start(0)
    probe_copy = remote(probes.at[0], prb.at[k], psem.at[0], psem.at[1], partner)
    probe_copy.start()
    for one in (2, 5, 6):
        local[one].wait()
    for there, at in (
        (has_right, (slice(0, T), far)),
        (has_below, (far, slice(0, T))),
        (has_right & has_below, (far, far)),
    ):
        @pl.when(jnp.logical_not(there))
        def _(at=at):
            for ext in exts:
                for c in range(2):
                    ext[(c,) + at] = jnp.zeros_like(ext[(c,) + at])

    oy, ox = off_ref[0, 0, k, 0], off_ref[0, 0, k, 1]

    def pick(shape_of, axis, low, wrap=False):
        here = lax.broadcasted_iota(jnp.int32, shape_of, axis)
        there = lax.broadcasted_iota(jnp.int32, shape_of, 1 - axis) + low
        if wrap:
            there = there & (E - 1)
        return jnp.where(here == there, 1.0, 0.0).astype(bf16)

    def window(s):
        by_row, by_col = pick((E, W), 1, oy), pick((W, E), 0, ox)
        result = []
        for c in range(2):
            strip = jnp.dot(by_row, exts[s][c], preferred_element_type=f32).astype(bf16)
            result.append(jnp.dot(strip, by_col, preferred_element_type=f32))
        return tuple(result)

    def transform(v, forward):
        lhs, rhs = (tab.at[0], tab.at[1]) if forward else (tab.at[1], tab.at[0])
        stacked = jnp.concatenate([v[0].astype(bf16), v[1].astype(bf16)], axis=0)
        mid = jnp.dot(lhs[...], stacked, preferred_element_type=f32).astype(bf16)
        wide = jnp.concatenate([mid[0:E], mid[E:]], axis=1)
        result = jnp.dot(wide, rhs[...], preferred_element_type=f32)
        return (result[:, 0:E], result[:, E:])

    modes = range(2)
    early(0)
    start(1)
    probe_copy.wait()
    arrive(0)

    def probe(m):
        return (prb[m, 0].astype(f32), prb[m, 1].astype(f32))

    def chirp():
        return (chp[0], chp[1])

    first = window(0)
    props = []
    for m in modes:
        spec = transform(cmul(probe(m), first), True)
        props.append(transform(cmul(chirp(), spec), False))
        if m == 0:
            early(1)
    arrive(1)
    second = window(1)
    fars = [transform(cmul(props[m], second), True) for m in modes]
    local[3].wait()
    local[4].wait()
    intensity = sum(f[0] * f[0] + f[1] * f[1] for f in fars)
    residual = 2.0 * wts[...] * (intensity - inten[...].astype(f32))
    backs = [transform((residual * fars[m][0], residual * fars[m][1]), False) for m in modes]

    alive = jnp.zeros((E, E), jnp.int32) + k < cnt_ref[0, 0]
    turn_y, turn_x = pick((E, E), 0, oy, True), pick((E, E), 1, ox, True)

    def finish(s, parts):
        for c in range(2):
            total = jnp.where(alive, parts[0][c] + parts[1][c], 0.0).astype(bf16)
            turned = jnp.dot(turn_y, total, preferred_element_type=f32).astype(bf16)
            gsend[s, c] = jnp.dot(turned, turn_x, preferred_element_type=f32).astype(bf16)

    give = remote(gsend.at[other], gpart, gsem.at[0], gsem.at[1], partner)
    finish(1, [conj_mul(props[m], backs[m]) for m in modes])

    @pl.when(k == 0)
    def _():
        give.start()

    half = E // 2

    def block(c, y, x, h, w):
        y0, x0 = y % E, x % E
        total = None
        for slot, values in (
            (k, gsend[k, c, y0 : y0 + h, x0 : x0 + w].astype(f32)),
            (other, gpart[c, y0 : y0 + h, x0 : x0 + w].astype(f32)),
        ):
            ypos = lax.broadcasted_iota(jnp.int32, (h, w), 0) + y
            xpos = lax.broadcasted_iota(jnp.int32, (h, w), 1) + x
            low_y, low_x = off_ref[0, 0, slot, 0], off_ref[0, 0, slot, 1]
            inside = (
                (ypos >= low_y) & (ypos < low_y + E) & (xpos >= low_x) & (xpos < low_x + E)
            )
            term = jnp.where(inside, values, 0.0)
            total = term if total is None else total + term
        return total

    def spans(start, stop):
        result = []
        while start < stop:
            end = min(stop, (start // half + 1) * half)
            result.append((start, end - start))
            start = end
        return result

    inner, outer = spans(0, T), spans(T, T + E)

    def fill(dst, c, ys, xs, y_base, x_base, dtype):
        for y, h in ys:
            for x, w in xs:
                dst[y - y_base : y - y_base + h, x - x_base : x - x_base + w] = block(
                    c, y, x, h, w
                ).astype(dtype)

    def push(i):
        src, dst, who = (
            (hd.at[0], rd.at[0], down), (hd.at[1], rd.at[1], right),
            (hb.at[0], rb.at[0], down), (hr.at[1], rr.at[1], right),
            (hb.at[1], rb.at[1], down), (hr.at[0], rr.at[0], right),
        )[i]
        return remote(src, dst, hsend.at[i], hrecv.at[i], who)

    both_out = has_right & has_below
    send_out = (both_out, both_out, has_below, has_right, has_below, has_right)

    def deliver_first():
        give.wait_recv()

        @pl.when(both_out)
        def _():
            for c in range(2):
                fill(hd.at[c], c, outer, outer, T, T, bf16)
                push(c).start()

        @pl.when(has_below)
        def _():
            fill(hb.at[0], 0, outer, inner, T, 0, bf16)
            push(2).start()

        @pl.when(has_right)
        def _():
            fill(hr.at[1], 1, inner, outer, 0, T, bf16)
            push(3).start()

        @pl.when(has_below)
        def _():
            fill(hb.at[1], 1, outer, inner, T, 0, bf16)

        @pl.when(has_right)
        def _():
            fill(hr.at[0], 0, inner, outer, 0, T, bf16)

    def deliver_second():
        @pl.when(has_below)
        def _():
            @pl.when(has_left)
            def _():
                push(1).wait_recv()
                hb[1, :, 0:E] = (hb[1, :, 0:E].astype(f32) + rd[1].astype(f32)).astype(bf16)

            push(4).start()

        @pl.when(has_right)
        def _():
            @pl.when(has_above)
            def _():
                push(0).wait_recv()
                hr[0, 0:E, :] = (hr[0, 0:E, :].astype(f32) + rd[0].astype(f32)).astype(bf16)

            push(5).start()

    gspecs = [transform(conj_mul(second, backs[m]), True) for m in modes]

    @pl.when(k == 1)
    def _():
        deliver_first()

    finish(0, [
        conj_mul(probe(m), transform(conj_mul(chirp(), gspecs[m]), False)) for m in modes
    ])

    @pl.when(k == 1)
    def _():
        give.start()

    @pl.when(k == 0)
    def _():
        deliver_first()

    deliver_second()
    for c in range(2):
        fill(out_ref.at[0, c], c, inner, inner, 0, 0, f32)

    for i, c, there, land, area in (
        (2, 0, has_above, rb, (near, slice(0, T))),
        (3, 1, has_left, rr, (slice(0, T), near)),
        (4, 1, has_above, rb, (near, slice(0, T))),
        (5, 0, has_left, rr, (slice(0, T), near)),
    ):
        @pl.when(there)
        def _(i=i, c=c, land=land, area=area):
            push(i).wait_recv()
            at = (0, c) + area
            out_ref[at] = out_ref[at] + land[c].astype(f32)

    for s in range(2):
        for piece in range(4):
            @pl.when(sends[piece])
            def _(s=s, piece=piece):
                halo(s, piece).wait_send()
        for piece in range(5):
            @pl.when(takes[piece])
            def _(s=s, piece=piece):
                relay(s, piece).wait_send()
        for core in range(2):
            @pl.when((k == core) & turn[core])
            def _(s=s, core=core):
                corner(s, core).wait_send()
    give.wait_send()
    for i in range(6):
        @pl.when(send_out[i])
        def _(i=i):
            push(i).wait_send()


def solution(mesh):
    rows_n, cols_n = mesh.shape["row"], mesh.shape["col"]

    def body(objects, probes, weights, counts, offsets, intensities):
        T, E = objects.shape[2], probes.shape[2]
        W = T + E
        any_space = pl.BlockSpec(memory_space=pl.ANY)
        smem = pl.BlockSpec(memory_space=pltpu.SMEM)
        dma = pltpu.SemaphoreType.DMA
        return pl.pallas_call(
            functools.partial(kernel, (rows_n, cols_n, T, E)),
            out_shape=jax.ShapeDtypeStruct((1, 2, T, T), f32),
            in_specs=[smem, smem] + [any_space] * 6,
            out_specs=pl.BlockSpec(memory_space=pltpu.VMEM),
            scratch_shapes=[
                pltpu.VMEM((2, W, W), bf16), pltpu.VMEM((2, W, W), bf16),
                pltpu.VMEM((2, 2, E, E), bf16), pltpu.VMEM((E, E), f32),
                pltpu.VMEM((E, E), bf16), pltpu.VMEM((2, 2 * E, 2 * E), bf16),
                pltpu.VMEM((2, E, E), f32),
                pltpu.VMEM((2, 2, E, E), bf16),
                pltpu.VMEM((2, E, E), bf16),
                pltpu.VMEM((2, E, T), bf16), pltpu.VMEM((2, T, E), bf16), pltpu.VMEM((2, E, E), bf16),
                pltpu.VMEM((2, E, T), bf16), pltpu.VMEM((2, T, E), bf16), pltpu.VMEM((2, E, E), bf16),
                dma((7,)), dma((2, 5)), dma((2, 5)), dma((2, 5)), dma((2, 5)),
                dma((2,)), dma((2,)), dma((6,)), dma((6,)),
            ],
            compiler_params=pltpu.CompilerParams(
                collective_id=0, has_side_effects=True, vmem_limit_bytes=63 * 1024 * 1024
            ),
            name="ptycho",
        )(
            offsets, counts, objects, probes, weights, intensities,
            jnp.asarray(dft_tables(E)), jnp.asarray(chirp_factor(E)),
        )

    in_specs = (
        P(None, None, ("grp", "row"), "col"),
        P(("grp", "slc"), None, None, None),
        P(),
        P(("grp", "row"), "col"),
        P(("grp", "row"), "col", None, None),
        P(("grp", "row"), "col", None, None, None),
    )
    out_specs = P("slc", None, ("grp", "row"), "col")
    return jax.shard_map(body, mesh=mesh, in_specs=in_specs, out_specs=out_specs, check_vma=False)
```

```python
import functools

import jax
import jax.numpy as jnp
import ml_dtypes
import numpy as np
from jax import lax
from jax.experimental import pallas as pl
from jax.experimental.pallas import tpu as pltpu
from jax.sharding import PartitionSpec as P

MESH = pl.DeviceIdType.MESH
fresnel = 0.5
f32 = jnp.float32
bf16 = jnp.bfloat16


def dft_tables(extent):
    counter = np.arange(extent, dtype=np.int64)
    product = counter[:, None] * counter[None, :] % extent
    angles = np.float32(2.0 * np.pi / extent) * product.astype(np.float32)
    norm_scale = np.float32(1.0 / np.sqrt(extent))
    real = (np.cos(angles) * norm_scale).astype(ml_dtypes.bfloat16)
    imag = (-np.sin(angles) * norm_scale).astype(ml_dtypes.bfloat16)
    plus = np.block([[real, -imag], [imag, real]])
    minus = np.block([[real, imag], [-imag, real]])
    return np.stack([plus, minus]).astype(ml_dtypes.bfloat16)


def chirp_factor(extent):
    counter = np.arange(extent, dtype=np.int64)
    signed = (counter + extent // 2) % extent - extent // 2
    squares = signed[:, None] ** 2 + signed[None, :] ** 2
    angles = np.float32(-np.pi * fresnel / extent) * squares.astype(np.float32)
    return np.stack([np.cos(angles), np.sin(angles)]).astype(np.float32)


def cmul(a, b):
    return (a[0] * b[0] - a[1] * b[1], a[0] * b[1] + a[1] * b[0])


def conj_mul(a, b):
    return (a[0] * b[0] + a[1] * b[1], a[0] * b[1] - a[1] * b[0])


def kernel(
    shape, off_ref, cnt_ref, obj, probes, weights, intens, tables, chirps, out_ref,
    ext1, ext2, prb, wts, inten, tab, chp, gsend, gpart,
    hb, hr, hd, rb, rr, rd, lsem, fsend, frecv, relsend, relrecv, psem, gsem, hsend, hrecv,
):
    rows_n, cols_n, T, E = shape
    row, col, k = lax.axis_index("row"), lax.axis_index("col"), lax.axis_index("slc")
    other = 1 - k
    exts = (ext1, ext2)
    has_right, has_left = col < cols_n - 1, col > 0
    has_below, has_above = row < rows_n - 1, row > 0
    partner = {"slc": other}
    up, down = {"row": row - 1}, {"row": row + 1}
    left, right = {"col": col - 1}, {"col": col + 1}
    sides = (
        (has_right, right), (has_left, left), (has_below, down), (has_above, up),
    )

    local = [
        pltpu.make_async_copy(obj.at[0], ext1.at[:, 0:T, 0:T], lsem.at[0]),
        pltpu.make_async_copy(obj.at[1], ext2.at[:, 0:T, 0:T], lsem.at[1]),
        pltpu.make_async_copy(probes.at[0], prb.at[k], lsem.at[2]),
        pltpu.make_async_copy(weights, wts, lsem.at[3]),
        pltpu.make_async_copy(intens.at[0, 0, k], inten, lsem.at[4]),
        pltpu.make_async_copy(tables, tab, lsem.at[5]),
        pltpu.make_async_copy(chirps, chp, lsem.at[6]),
    ]
    for one in local:
        one.start()

    barrier = pltpu.get_barrier_semaphore()
    pl.semaphore_signal(barrier, inc=1, device_id=partner, device_id_type=MESH)
    for there, who in sides:
        @pl.when(there)
        def _(who=who):
            pl.semaphore_signal(barrier, inc=1, device_id=who, device_id_type=MESH)
    peers = 1
    for there, _ in sides:
        peers = peers + there.astype(jnp.int32)
    pl.semaphore_wait(barrier, peers)

    def remote(src, dst, ssem, rsem, who):
        return pltpu.make_async_remote_copy(
            src_ref=src, dst_ref=dst, send_sem=ssem, recv_sem=rsem,
            device_id=who, device_id_type=MESH,
        )

    W = T + E
    near, rest, far = slice(0, E), slice(E, T), slice(T, W)
    places = ((near, far), (far, near), (rest, far), (far, rest), (far, far))
    sources = ((near, near), (near, near), (rest, near), (near, rest))
    sends = (has_left, has_above, has_left, has_above)
    takes = (has_right, has_below, has_right, has_below, has_right & has_below)
    targets = (left, up, left, up)
    turn = (has_above & has_right, has_left & has_below)

    def halo(s, piece):
        return remote(
            obj.at[(s, k) + sources[piece]], exts[s].at[(k,) + places[piece]],
            fsend.at[s, piece], frecv.at[s, piece], targets[piece],
        )

    def corner(s, core):
        return remote(
            exts[s].at[(core,) + places[core]], exts[s].at[(core,) + places[4]],
            fsend.at[s, 4], frecv.at[s, 4], targets[1 - core],
        )

    def relay(s, piece):
        region = exts[s].at[(k,) + places[piece]]
        return remote(region, region, relsend.at[s, piece], relrecv.at[s, piece], partner)

    def start(s):
        for piece in range(4):
            @pl.when(sends[piece])
            def _(piece=piece):
                halo(s, piece).start()

    def hand_over(s, piece):
        @pl.when(takes[piece])
        def _():
            if piece < 4:
                halo(s, piece).wait_recv()
            else:
                corner(s, 0).wait_recv()
            relay(s, piece).start()

    def early(s):
        for core in range(2):
            @pl.when(k == core)
            def _(core=core):
                hand_over(s, core)

                @pl.when(turn[core])
                def _():
                    corner(s, core).start()

    def other_corner(s):
        for core in range(2):
            @pl.when(k == core)
            def _(core=core):
                hand_over(s, 1 - core)

    def landed(s, pieces):
        for piece in pieces:
            @pl.when(takes[piece])
            def _(piece=piece):
                relay(s, piece).wait_recv()

    start(0)
    probe_copy = remote(probes.at[0], prb.at[k], psem.at[0], psem.at[1], partner)
    probe_copy.start()
    for one in (2, 5, 6):
        local[one].wait()
    for there, at in (
        (has_right, (slice(0, T), far)),
        (has_below, (far, slice(0, T))),
        (has_right & has_below, (far, far)),
    ):
        @pl.when(jnp.logical_not(there))
        def _(at=at):
            for ext in exts:
                for c in range(2):
                    ext[(c,) + at] = jnp.zeros_like(ext[(c,) + at])

    oy, ox = off_ref[0, 0, k, 0], off_ref[0, 0, k, 1]

    def pick(shape_of, axis, low, wrap=False):
        here = lax.broadcasted_iota(jnp.int32, shape_of, axis)
        there = lax.broadcasted_iota(jnp.int32, shape_of, 1 - axis) + low
        if wrap:
            there = there & (E - 1)
        return jnp.where(here == there, 1.0, 0.0).astype(bf16)

    low = slice(0, T)
    row_low, row_far = pick((E, T), 1, oy), pick((E, E), 1, oy - T)
    col_low, col_far = pick((T, E), 0, ox), pick((E, E), 0, ox - T)

    def part(s, by_row, by_col, at):
        result = []
        for c in range(2):
            strip = jnp.dot(by_row, exts[s][(c,) + at], preferred_element_type=f32)
            result.append(jnp.dot(strip.astype(bf16), by_col, preferred_element_type=f32))
        return tuple(result)

    def plus(x, y):
        return (x[0] + y[0], x[1] + y[1])

    def window(s):
        for piece in (2, 3):
            hand_over(s, piece)
        landed(s, (0, 1, 2, 3))
        sides = plus(
            part(s, row_low, col_far, (low, far)), part(s, row_far, col_low, (far, low))
        )
        sides = plus(owns[s], sides)
        hand_over(s, 4)
        landed(s, (4,))
        return plus(sides, part(s, row_far, col_far, (far, far)))

    def transform(v, forward):
        lhs, rhs = (tab.at[0], tab.at[1]) if forward else (tab.at[1], tab.at[0])
        stacked = jnp.concatenate([v[0].astype(bf16), v[1].astype(bf16)], axis=0)
        mid = jnp.dot(lhs[...], stacked, preferred_element_type=f32).astype(bf16)
        wide = jnp.concatenate([mid[0:E], mid[E:]], axis=1)
        result = jnp.dot(wide, rhs[...], preferred_element_type=f32)
        return (result[:, 0:E], result[:, E:])

    modes = range(2)
    owns = []
    for s in range(2):
        local[s].wait()
        owns.append(part(s, row_low, col_low, (low, low)))
    early(0)
    start(1)
    other_corner(0)
    probe_copy.wait()

    def probe(m):
        return (prb[m, 0].astype(f32), prb[m, 1].astype(f32))

    def chirp():
        return (chp[0], chp[1])

    first = window(0)
    props = []
    for m in modes:
        spec = transform(cmul(probe(m), first), True)
        props.append(transform(cmul(chirp(), spec), False))
        if m == 0:
            early(1)
            other_corner(1)
    second = window(1)
    fars = [transform(cmul(props[m], second), True) for m in modes]
    local[3].wait()
    local[4].wait()
    intensity = sum(f[0] * f[0] + f[1] * f[1] for f in fars)
    residual = 2.0 * wts[...] * (intensity - inten[...].astype(f32))
    backs = [transform((residual * fars[m][0], residual * fars[m][1]), False) for m in modes]

    alive = jnp.zeros((E, E), jnp.int32) + k < cnt_ref[0, 0]
    turn_y, turn_x = pick((E, E), 0, oy, True), pick((E, E), 1, ox, True)

    def finish(s, parts):
        for c in range(2):
            total = jnp.where(alive, parts[0][c] + parts[1][c], 0.0).astype(bf16)
            turned = jnp.dot(turn_y, total, preferred_element_type=f32).astype(bf16)
            gsend[s, c] = jnp.dot(turned, turn_x, preferred_element_type=f32).astype(bf16)

    give = remote(gsend.at[other], gpart, gsem.at[0], gsem.at[1], partner)
    finish(1, [conj_mul(props[m], backs[m]) for m in modes])

    @pl.when(k == 0)
    def _():
        give.start()

    half = E // 2

    def block(c, y, x, h, w):
        y0, x0 = y % E, x % E
        total = None
        for slot, values in (
            (k, gsend[k, c, y0 : y0 + h, x0 : x0 + w].astype(f32)),
            (other, gpart[c, y0 : y0 + h, x0 : x0 + w].astype(f32)),
        ):
            ypos = lax.broadcasted_iota(jnp.int32, (h, w), 0) + y
            xpos = lax.broadcasted_iota(jnp.int32, (h, w), 1) + x
            low_y, low_x = off_ref[0, 0, slot, 0], off_ref[0, 0, slot, 1]
            inside = (
                (ypos >= low_y) & (ypos < low_y + E) & (xpos >= low_x) & (xpos < low_x + E)
            )
            term = jnp.where(inside, values, 0.0)
            total = term if total is None else total + term
        return total

    def spans(start, stop):
        result = []
        while start < stop:
            end = min(stop, (start // half + 1) * half)
            result.append((start, end - start))
            start = end
        return result

    inner, outer = spans(0, T), spans(T, T + E)

    def fill(dst, c, ys, xs, y_base, x_base, dtype):
        for y, h in ys:
            for x, w in xs:
                dst[y - y_base : y - y_base + h, x - x_base : x - x_base + w] = block(
                    c, y, x, h, w
                ).astype(dtype)

    def push(i):
        src, dst, who = (
            (hd.at[0], rd.at[0], down), (hd.at[1], rd.at[1], right),
            (hb.at[0], rb.at[0], down), (hr.at[1], rr.at[1], right),
            (hb.at[1], rb.at[1], down), (hr.at[0], rr.at[0], right),
        )[i]
        return remote(src, dst, hsend.at[i], hrecv.at[i], who)

    both_out = has_right & has_below
    send_out = (both_out, both_out, has_below, has_right, has_below, has_right)

    def deliver_first():
        give.wait_recv()

        @pl.when(both_out)
        def _():
            for c in range(2):
                fill(hd.at[c], c, outer, outer, T, T, bf16)
                push(c).start()

        @pl.when(has_below)
        def _():
            fill(hb.at[0], 0, outer, inner, T, 0, bf16)
            push(2).start()

        @pl.when(has_right)
        def _():
            fill(hr.at[1], 1, inner, outer, 0, T, bf16)
            push(3).start()

        @pl.when(has_below)
        def _():
            fill(hb.at[1], 1, outer, inner, T, 0, bf16)

        @pl.when(has_right)
        def _():
            fill(hr.at[0], 0, inner, outer, 0, T, bf16)

    def deliver_second():
        @pl.when(has_below)
        def _():
            @pl.when(has_left)
            def _():
                push(1).wait_recv()
                hb[1, :, 0:E] = (hb[1, :, 0:E].astype(f32) + rd[1].astype(f32)).astype(bf16)

            push(4).start()

        @pl.when(has_right)
        def _():
            @pl.when(has_above)
            def _():
                push(0).wait_recv()
                hr[0, 0:E, :] = (hr[0, 0:E, :].astype(f32) + rd[0].astype(f32)).astype(bf16)

            push(5).start()

    gspecs = [transform(conj_mul(second, backs[m]), True) for m in modes]

    @pl.when(k == 1)
    def _():
        deliver_first()

    finish(0, [
        conj_mul(probe(m), transform(conj_mul(chirp(), gspecs[m]), False)) for m in modes
    ])

    @pl.when(k == 1)
    def _():
        give.start()

    @pl.when(k == 0)
    def _():
        deliver_first()

    deliver_second()
    for c in range(2):
        fill(out_ref.at[0, c], c, inner, inner, 0, 0, f32)

    for i, c, there, land, area in (
        (2, 0, has_above, rb, (near, slice(0, T))),
        (3, 1, has_left, rr, (slice(0, T), near)),
        (4, 1, has_above, rb, (near, slice(0, T))),
        (5, 0, has_left, rr, (slice(0, T), near)),
    ):
        @pl.when(there)
        def _(i=i, c=c, land=land, area=area):
            push(i).wait_recv()
            at = (0, c) + area
            out_ref[at] = out_ref[at] + land[c].astype(f32)

    for s in range(2):
        for piece in range(4):
            @pl.when(sends[piece])
            def _(s=s, piece=piece):
                halo(s, piece).wait_send()
        for piece in range(5):
            @pl.when(takes[piece])
            def _(s=s, piece=piece):
                relay(s, piece).wait_send()
        for core in range(2):
            @pl.when((k == core) & turn[core])
            def _(s=s, core=core):
                corner(s, core).wait_send()
    give.wait_send()
    for i in range(6):
        @pl.when(send_out[i])
        def _(i=i):
            push(i).wait_send()


def solution(mesh):
    rows_n, cols_n = mesh.shape["row"], mesh.shape["col"]

    def body(objects, probes, weights, counts, offsets, intensities):
        T, E = objects.shape[2], probes.shape[2]
        W = T + E
        any_space = pl.BlockSpec(memory_space=pl.ANY)
        smem = pl.BlockSpec(memory_space=pltpu.SMEM)
        dma = pltpu.SemaphoreType.DMA
        return pl.pallas_call(
            functools.partial(kernel, (rows_n, cols_n, T, E)),
            out_shape=jax.ShapeDtypeStruct((1, 2, T, T), f32),
            in_specs=[smem, smem] + [any_space] * 6,
            out_specs=pl.BlockSpec(memory_space=pltpu.VMEM),
            scratch_shapes=[
                pltpu.VMEM((2, W, W), bf16), pltpu.VMEM((2, W, W), bf16),
                pltpu.VMEM((2, 2, E, E), bf16), pltpu.VMEM((E, E), f32),
                pltpu.VMEM((E, E), bf16), pltpu.VMEM((2, 2 * E, 2 * E), bf16),
                pltpu.VMEM((2, E, E), f32),
                pltpu.VMEM((2, 2, E, E), bf16),
                pltpu.VMEM((2, E, E), bf16),
                pltpu.VMEM((2, E, T), bf16), pltpu.VMEM((2, T, E), bf16), pltpu.VMEM((2, E, E), bf16),
                pltpu.VMEM((2, E, T), bf16), pltpu.VMEM((2, T, E), bf16), pltpu.VMEM((2, E, E), bf16),
                dma((7,)), dma((2, 5)), dma((2, 5)), dma((2, 5)), dma((2, 5)),
                dma((2,)), dma((2,)), dma((6,)), dma((6,)),
            ],
            compiler_params=pltpu.CompilerParams(
                collective_id=0, has_side_effects=True, vmem_limit_bytes=63 * 1024 * 1024
            ),
            name="ptycho",
        )(
            offsets, counts, objects, probes, weights, intensities,
            jnp.asarray(dft_tables(E)), jnp.asarray(chirp_factor(E)),
        )

    in_specs = (
        P(None, None, ("grp", "row"), "col"),
        P(("grp", "slc"), None, None, None),
        P(),
        P(("grp", "row"), "col"),
        P(("grp", "row"), "col", None, None),
        P(("grp", "row"), "col", None, None, None),
    )
    out_specs = P("slc", None, ("grp", "row"), "col")
    return jax.shard_map(body, mesh=mesh, in_specs=in_specs, out_specs=out_specs, check_vma=False)
```

```python
import functools

import jax
import jax.numpy as jnp
import ml_dtypes
import numpy as np
from jax import lax
from jax.experimental import pallas as pl
from jax.experimental.pallas import tpu as pltpu
from jax.sharding import PartitionSpec as P

MESH = pl.DeviceIdType.MESH
fresnel = 0.5
f32 = jnp.float32
bf16 = jnp.bfloat16


def dft_tables(extent):
    counter = np.arange(extent, dtype=np.int64)
    product = counter[:, None] * counter[None, :] % extent
    angles = np.float32(2.0 * np.pi / extent) * product.astype(np.float32)
    norm_scale = np.float32(1.0 / np.sqrt(extent))
    real = (np.cos(angles) * norm_scale).astype(ml_dtypes.bfloat16)
    imag = (-np.sin(angles) * norm_scale).astype(ml_dtypes.bfloat16)
    plus = np.block([[real, -imag], [imag, real]])
    minus = np.block([[real, imag], [-imag, real]])
    return np.stack([plus, minus]).astype(ml_dtypes.bfloat16)


def chirp_factor(extent):
    counter = np.arange(extent, dtype=np.int64)
    signed = (counter + extent // 2) % extent - extent // 2
    squares = signed[:, None] ** 2 + signed[None, :] ** 2
    angles = np.float32(-np.pi * fresnel / extent) * squares.astype(np.float32)
    return np.stack([np.cos(angles), np.sin(angles)]).astype(np.float32)


def cmul(a, b):
    return (a[0] * b[0] - a[1] * b[1], a[0] * b[1] + a[1] * b[0])


def conj_mul(a, b):
    return (a[0] * b[0] + a[1] * b[1], a[0] * b[1] - a[1] * b[0])


def kernel(
    shape, off_ref, cnt_ref, obj, probes, weights, intens, tables, chirps, out_ref,
    ext1, ext2, prb, wts, inten, tab, chp, gsend, gpart,
    hb, hr, hd, rb, rr, rd, lsem, fsend, frecv, relsend, relrecv, psem, gsem, hsend, hrecv,
):
    rows_n, cols_n, T, E = shape
    row, col, k = lax.axis_index("row"), lax.axis_index("col"), lax.axis_index("slc")
    other = 1 - k
    exts = (ext1, ext2)
    has_right, has_left = col < cols_n - 1, col > 0
    has_below, has_above = row < rows_n - 1, row > 0
    partner = {"slc": other}
    up, down = {"row": row - 1}, {"row": row + 1}
    left, right = {"col": col - 1}, {"col": col + 1}
    sides = (
        (has_right, right), (has_left, left), (has_below, down), (has_above, up),
    )

    local = [
        pltpu.make_async_copy(obj.at[0], ext1.at[:, 0:T, 0:T], lsem.at[0]),
        pltpu.make_async_copy(obj.at[1], ext2.at[:, 0:T, 0:T], lsem.at[1]),
        pltpu.make_async_copy(probes.at[0], prb.at[k], lsem.at[2]),
        pltpu.make_async_copy(weights, wts, lsem.at[3]),
        pltpu.make_async_copy(intens.at[0, 0, k], inten, lsem.at[4]),
        pltpu.make_async_copy(tables, tab, lsem.at[5]),
        pltpu.make_async_copy(chirps, chp, lsem.at[6]),
    ]
    for one in local:
        one.start()

    barrier = pltpu.get_barrier_semaphore()
    pl.semaphore_signal(barrier, inc=1, device_id=partner, device_id_type=MESH)
    for there, who in sides:
        @pl.when(there)
        def _(who=who):
            pl.semaphore_signal(barrier, inc=1, device_id=who, device_id_type=MESH)
    peers = 1
    for there, _ in sides:
        peers = peers + there.astype(jnp.int32)
    pl.semaphore_wait(barrier, peers)

    def remote(src, dst, ssem, rsem, who):
        return pltpu.make_async_remote_copy(
            src_ref=src, dst_ref=dst, send_sem=ssem, recv_sem=rsem,
            device_id=who, device_id_type=MESH,
        )

    W = T + E
    near, rest, far = slice(0, E), slice(E, T), slice(T, W)
    places = ((near, far), (far, near), (rest, far), (far, rest), (far, far))
    sources = ((near, near), (near, near), (rest, near), (near, rest))
    sends = (has_left, has_above, has_left, has_above)
    takes = (has_right, has_below, has_right, has_below, has_right & has_below)
    targets = (left, up, left, up)
    turn = (has_above & has_right, has_left & has_below)

    def halo(s, piece):
        return remote(
            obj.at[(s, k) + sources[piece]], exts[s].at[(k,) + places[piece]],
            fsend.at[s, piece], frecv.at[s, piece], targets[piece],
        )

    def corner(s, core):
        return remote(
            exts[s].at[(core,) + places[core]], exts[s].at[(core,) + places[4]],
            fsend.at[s, 4], frecv.at[s, 4], targets[1 - core],
        )

    def relay(s, piece):
        region = exts[s].at[(k,) + places[piece]]
        return remote(region, region, relsend.at[s, piece], relrecv.at[s, piece], partner)

    def start(s):
        for piece in range(4):
            @pl.when(sends[piece])
            def _(piece=piece):
                halo(s, piece).start()

    def hand_over(s, piece):
        @pl.when(takes[piece])
        def _():
            if piece < 4:
                halo(s, piece).wait_recv()
            else:
                corner(s, 0).wait_recv()
            relay(s, piece).start()

    def early(s):
        for core in range(2):
            @pl.when(k == core)
            def _(core=core):
                hand_over(s, core)

                @pl.when(turn[core])
                def _():
                    corner(s, core).start()

    def other_corner(s):
        for core in range(2):
            @pl.when(k == core)
            def _(core=core):
                hand_over(s, 1 - core)

    def landed(s, pieces):
        for piece in pieces:
            @pl.when(takes[piece])
            def _(piece=piece):
                relay(s, piece).wait_recv()

    start(0)
    probe_copy = remote(probes.at[0], prb.at[k], psem.at[0], psem.at[1], partner)
    probe_copy.start()
    for one in (2, 5, 6):
        local[one].wait()
    for there, at in (
        (has_right, (slice(0, T), far)),
        (has_below, (far, slice(0, T))),
        (has_right & has_below, (far, far)),
    ):
        @pl.when(jnp.logical_not(there))
        def _(at=at):
            for ext in exts:
                for c in range(2):
                    ext[(c,) + at] = jnp.zeros_like(ext[(c,) + at])

    oy, ox = off_ref[0, 0, k, 0], off_ref[0, 0, k, 1]

    def pick(shape_of, axis, low, wrap=False):
        here = lax.broadcasted_iota(jnp.int32, shape_of, axis)
        there = lax.broadcasted_iota(jnp.int32, shape_of, 1 - axis) + low
        if wrap:
            there = there & (E - 1)
        return jnp.where(here == there, 1.0, 0.0).astype(bf16)

    low = slice(0, T)
    row_low, row_far = pick((E, T), 1, oy), pick((E, E), 1, oy - T)
    col_low, col_far = pick((T, E), 0, ox), pick((E, E), 0, ox - T)

    def part(s, by_row, by_col, at):
        result = []
        for c in range(2):
            strip = jnp.dot(by_row, exts[s][(c,) + at], preferred_element_type=f32)
            result.append(jnp.dot(strip.astype(bf16), by_col, preferred_element_type=f32))
        return tuple(result)

    def plus(x, y):
        return (x[0] + y[0], x[1] + y[1])

    def window(s):
        for piece in (2, 3):
            hand_over(s, piece)
        landed(s, (0, 1, 2, 3))
        sides = plus(
            part(s, row_low, col_far, (low, far)), part(s, row_far, col_low, (far, low))
        )
        sides = plus(owns[s], sides)
        hand_over(s, 4)
        landed(s, (4,))
        return plus(sides, part(s, row_far, col_far, (far, far)))

    def transform(v, forward):
        lhs, rhs = (tab.at[0], tab.at[1]) if forward else (tab.at[1], tab.at[0])
        stacked = jnp.concatenate([v[0].astype(bf16), v[1].astype(bf16)], axis=0)
        mid = jnp.dot(lhs[...], stacked, preferred_element_type=f32).astype(bf16)
        wide = jnp.concatenate([mid[0:E], mid[E:]], axis=1)
        result = jnp.dot(wide, rhs[...], preferred_element_type=f32)
        return (result[:, 0:E], result[:, E:])

    modes = range(2)
    owns = []
    for s in range(2):
        local[s].wait()
        owns.append(part(s, row_low, col_low, (low, low)))
    early(0)
    start(1)
    other_corner(0)
    probe_copy.wait()

    def probe(m):
        return (prb[m, 0].astype(f32), prb[m, 1].astype(f32))

    def chirp():
        return (chp[0], chp[1])

    first = window(0)
    props = []
    for m in modes:
        spec = transform(cmul(probe(m), first), True)
        props.append(transform(cmul(chirp(), spec), False))
        if m == 0:
            early(1)
            other_corner(1)
    second = window(1)
    fars = [transform(cmul(props[m], second), True) for m in modes]
    local[3].wait()
    local[4].wait()
    intensity = sum(f[0] * f[0] + f[1] * f[1] for f in fars)
    residual = 2.0 * wts[...] * (intensity - inten[...].astype(f32))
    backs = [transform((residual * fars[m][0], residual * fars[m][1]), False) for m in modes]

    alive = jnp.zeros((E, E), jnp.int32) + k < cnt_ref[0, 0]
    turn_y, turn_x = pick((E, E), 0, oy, True), pick((E, E), 1, ox, True)

    def give(c):
        return remote(gsend.at[other, c], gpart.at[c], gsem.at[c], gsem.at[2 + c], partner)

    def finish(s, parts):
        for c in range(2):
            total = jnp.where(alive, parts[0][c] + parts[1][c], 0.0).astype(bf16)
            turned = jnp.dot(turn_y, total, preferred_element_type=f32).astype(bf16)
            gsend[s, c] = jnp.dot(turned, turn_x, preferred_element_type=f32).astype(bf16)

            @pl.when(k == 1 - s)
            def _():
                give(c).start()

    finish(1, [conj_mul(props[m], backs[m]) for m in modes])

    half = E // 2

    def block(c, y, x, h, w):
        y0, x0 = y % E, x % E
        total = None
        for slot, values in (
            (k, gsend[k, c, y0 : y0 + h, x0 : x0 + w].astype(f32)),
            (other, gpart[c, y0 : y0 + h, x0 : x0 + w].astype(f32)),
        ):
            ypos = lax.broadcasted_iota(jnp.int32, (h, w), 0) + y
            xpos = lax.broadcasted_iota(jnp.int32, (h, w), 1) + x
            low_y, low_x = off_ref[0, 0, slot, 0], off_ref[0, 0, slot, 1]
            inside = (
                (ypos >= low_y) & (ypos < low_y + E) & (xpos >= low_x) & (xpos < low_x + E)
            )
            term = jnp.where(inside, values, 0.0)
            total = term if total is None else total + term
        return total

    def spans(start, stop):
        result = []
        while start < stop:
            end = min(stop, (start // half + 1) * half)
            result.append((start, end - start))
            start = end
        return result

    inner, outer = spans(0, T), spans(T, T + E)

    def fill(dst, c, ys, xs, y_base, x_base, dtype):
        for y, h in ys:
            for x, w in xs:
                dst[y - y_base : y - y_base + h, x - x_base : x - x_base + w] = block(
                    c, y, x, h, w
                ).astype(dtype)

    def push(i):
        src, dst, who = (
            (hd.at[0], rd.at[0], down), (hd.at[1], rd.at[1], right),
            (hb.at[0], rb.at[0], down), (hr.at[1], rr.at[1], right),
            (hb.at[1], rb.at[1], down), (hr.at[0], rr.at[0], right),
        )[i]
        return remote(src, dst, hsend.at[i], hrecv.at[i], who)

    both_out = has_right & has_below
    send_out = (both_out, both_out, has_below, has_right, has_below, has_right)

    def deliver_first():
        for c in range(2):
            give(c).wait_recv()

            @pl.when(both_out)
            def _():
                fill(hd.at[c], c, outer, outer, T, T, bf16)
                push(c).start()

        @pl.when(has_below)
        def _():
            fill(hb.at[0], 0, outer, inner, T, 0, bf16)
            push(2).start()

        @pl.when(has_right)
        def _():
            fill(hr.at[1], 1, inner, outer, 0, T, bf16)
            push(3).start()

    def deliver_second():
        @pl.when(has_below)
        def _():
            fill(hb.at[1], 1, outer, inner, T, 0, bf16)

            @pl.when(has_left)
            def _():
                push(1).wait_recv()
                hb[1, :, 0:E] = (hb[1, :, 0:E].astype(f32) + rd[1].astype(f32)).astype(bf16)

            push(4).start()

        @pl.when(has_right)
        def _():
            fill(hr.at[0], 0, inner, outer, 0, T, bf16)

            @pl.when(has_above)
            def _():
                push(0).wait_recv()
                hr[0, 0:E, :] = (hr[0, 0:E, :].astype(f32) + rd[0].astype(f32)).astype(bf16)

            push(5).start()

    gspecs = [transform(conj_mul(second, backs[m]), True) for m in modes]

    @pl.when(k == 1)
    def _():
        deliver_first()

    finish(0, [
        conj_mul(probe(m), transform(conj_mul(chirp(), gspecs[m]), False)) for m in modes
    ])

    @pl.when(k == 0)
    def _():
        deliver_first()

    deliver_second()
    for c in range(2):
        fill(out_ref.at[0, c], c, inner, inner, 0, 0, f32)

    for i, c, there, land, area in (
        (2, 0, has_above, rb, (near, slice(0, T))),
        (3, 1, has_left, rr, (slice(0, T), near)),
        (4, 1, has_above, rb, (near, slice(0, T))),
        (5, 0, has_left, rr, (slice(0, T), near)),
    ):
        @pl.when(there)
        def _(i=i, c=c, land=land, area=area):
            push(i).wait_recv()
            at = (0, c) + area
            out_ref[at] = out_ref[at] + land[c].astype(f32)

    for s in range(2):
        for piece in range(4):
            @pl.when(sends[piece])
            def _(s=s, piece=piece):
                halo(s, piece).wait_send()
        for piece in range(5):
            @pl.when(takes[piece])
            def _(s=s, piece=piece):
                relay(s, piece).wait_send()
        for core in range(2):
            @pl.when((k == core) & turn[core])
            def _(s=s, core=core):
                corner(s, core).wait_send()
    for c in range(2):
        give(c).wait_send()
    for i in range(6):
        @pl.when(send_out[i])
        def _(i=i):
            push(i).wait_send()


def solution(mesh):
    rows_n, cols_n = mesh.shape["row"], mesh.shape["col"]

    def body(objects, probes, weights, counts, offsets, intensities):
        T, E = objects.shape[2], probes.shape[2]
        W = T + E
        any_space = pl.BlockSpec(memory_space=pl.ANY)
        smem = pl.BlockSpec(memory_space=pltpu.SMEM)
        dma = pltpu.SemaphoreType.DMA
        return pl.pallas_call(
            functools.partial(kernel, (rows_n, cols_n, T, E)),
            out_shape=jax.ShapeDtypeStruct((1, 2, T, T), f32),
            in_specs=[smem, smem] + [any_space] * 6,
            out_specs=pl.BlockSpec(memory_space=pltpu.VMEM),
            scratch_shapes=[
                pltpu.VMEM((2, W, W), bf16), pltpu.VMEM((2, W, W), bf16),
                pltpu.VMEM((2, 2, E, E), bf16), pltpu.VMEM((E, E), f32),
                pltpu.VMEM((E, E), bf16), pltpu.VMEM((2, 2 * E, 2 * E), bf16),
                pltpu.VMEM((2, E, E), f32),
                pltpu.VMEM((2, 2, E, E), bf16),
                pltpu.VMEM((2, E, E), bf16),
                pltpu.VMEM((2, E, T), bf16), pltpu.VMEM((2, T, E), bf16), pltpu.VMEM((2, E, E), bf16),
                pltpu.VMEM((2, E, T), bf16), pltpu.VMEM((2, T, E), bf16), pltpu.VMEM((2, E, E), bf16),
                dma((7,)), dma((2, 5)), dma((2, 5)), dma((2, 5)), dma((2, 5)),
                dma((2,)), dma((4,)), dma((6,)), dma((6,)),
            ],
            compiler_params=pltpu.CompilerParams(
                collective_id=0, has_side_effects=True, vmem_limit_bytes=63 * 1024 * 1024
            ),
            name="ptycho",
        )(
            offsets, counts, objects, probes, weights, intensities,
            jnp.asarray(dft_tables(E)), jnp.asarray(chirp_factor(E)),
        )

    in_specs = (
        P(None, None, ("grp", "row"), "col"),
        P(("grp", "slc"), None, None, None),
        P(),
        P(("grp", "row"), "col"),
        P(("grp", "row"), "col", None, None),
        P(("grp", "row"), "col", None, None, None),
    )
    out_specs = P("slc", None, ("grp", "row"), "col")
    return jax.shard_map(body, mesh=mesh, in_specs=in_specs, out_specs=out_specs, check_vma=False)
```

```python
import functools

import jax
import jax.numpy as jnp
import ml_dtypes
import numpy as np
from jax import lax
from jax.experimental import pallas as pl
from jax.experimental.pallas import tpu as pltpu
from jax.sharding import PartitionSpec as P

MESH = pl.DeviceIdType.MESH
fresnel = 0.5
f32 = jnp.float32
bf16 = jnp.bfloat16


def dft_tables(extent):
    counter = np.arange(extent, dtype=np.int64)
    product = counter[:, None] * counter[None, :] % extent
    angles = np.float32(2.0 * np.pi / extent) * product.astype(np.float32)
    norm_scale = np.float32(1.0 / np.sqrt(extent))
    real = (np.cos(angles) * norm_scale).astype(ml_dtypes.bfloat16)
    imag = (-np.sin(angles) * norm_scale).astype(ml_dtypes.bfloat16)
    plus = np.block([[real, -imag], [imag, real]])
    minus = np.block([[real, imag], [-imag, real]])
    return np.stack([plus, minus]).astype(ml_dtypes.bfloat16)


def chirp_factor(extent):
    counter = np.arange(extent, dtype=np.int64)
    signed = (counter + extent // 2) % extent - extent // 2
    squares = signed[:, None] ** 2 + signed[None, :] ** 2
    angles = np.float32(-np.pi * fresnel / extent) * squares.astype(np.float32)
    return np.stack([np.cos(angles), np.sin(angles)]).astype(np.float32)


def cmul(a, b):
    return (a[0] * b[0] - a[1] * b[1], a[0] * b[1] + a[1] * b[0])


def conj_mul(a, b):
    return (a[0] * b[0] + a[1] * b[1], a[0] * b[1] - a[1] * b[0])


def kernel(
    shape, off_ref, cnt_ref, obj, probes, weights, intens, tables, chirps, out_ref,
    ext1, ext2, prb, wts, inten, tab, chp, gsend, gpart,
    hb, hr, hd, rb, rr, rd, lsem, fsend, frecv, relsend, relrecv, psem, gsem, hsend, hrecv,
):
    rows_n, cols_n, T, E = shape
    row, col, k = lax.axis_index("row"), lax.axis_index("col"), lax.axis_index("slc")
    other = 1 - k
    exts = (ext1, ext2)
    has_right, has_left = col < cols_n - 1, col > 0
    has_below, has_above = row < rows_n - 1, row > 0
    partner = {"slc": other}
    up, down = {"row": row - 1}, {"row": row + 1}
    left, right = {"col": col - 1}, {"col": col + 1}
    sides = (
        (has_right, right), (has_left, left), (has_below, down), (has_above, up),
    )

    local = [
        pltpu.make_async_copy(obj.at[0], ext1.at[:, 0:T, 0:T], lsem.at[0]),
        pltpu.make_async_copy(obj.at[1], ext2.at[:, 0:T, 0:T], lsem.at[1]),
        pltpu.make_async_copy(probes.at[0], prb.at[k], lsem.at[2]),
        pltpu.make_async_copy(weights, wts, lsem.at[3]),
        pltpu.make_async_copy(intens.at[0, 0, k], inten, lsem.at[4]),
        pltpu.make_async_copy(tables, tab, lsem.at[5]),
        pltpu.make_async_copy(chirps, chp, lsem.at[6]),
    ]
    for one in local:
        one.start()

    barrier = pltpu.get_barrier_semaphore()
    pl.semaphore_signal(barrier, inc=1, device_id=partner, device_id_type=MESH)
    for there, who in sides:
        @pl.when(there)
        def _(who=who):
            pl.semaphore_signal(barrier, inc=1, device_id=who, device_id_type=MESH)
    peers = 1
    for there, _ in sides:
        peers = peers + there.astype(jnp.int32)
    pl.semaphore_wait(barrier, peers)

    def remote(src, dst, ssem, rsem, who):
        return pltpu.make_async_remote_copy(
            src_ref=src, dst_ref=dst, send_sem=ssem, recv_sem=rsem,
            device_id=who, device_id_type=MESH,
        )

    W = T + E
    near, rest, far = slice(0, E), slice(E, T), slice(T, W)
    places = ((near, far), (far, near), (rest, far), (far, rest), (far, far))
    sources = ((near, near), (near, near), (rest, near), (near, rest))
    sends = (has_left, has_above, has_left, has_above)
    takes = (has_right, has_below, has_right, has_below, has_right & has_below)
    targets = (left, up, left, up)
    turn = (has_above & has_right, has_left & has_below)

    def halo(s, piece):
        return remote(
            obj.at[(s, k) + sources[piece]], exts[s].at[(k,) + places[piece]],
            fsend.at[s, piece], frecv.at[s, piece], targets[piece],
        )

    def corner(s, core):
        return remote(
            exts[s].at[(core,) + places[core]], exts[s].at[(core,) + places[4]],
            fsend.at[s, 4], frecv.at[s, 4], targets[1 - core],
        )

    def relay(s, piece):
        region = exts[s].at[(k,) + places[piece]]
        return remote(region, region, relsend.at[s, piece], relrecv.at[s, piece], partner)

    def start(s, link=None):
        for piece in range(4):
            @pl.when(sends[piece] if link is None else sends[piece] & (link == piece % 2))
            def _(piece=piece):
                halo(s, piece).start()

    def hand_over(s, piece):
        @pl.when(takes[piece])
        def _():
            if piece < 4:
                halo(s, piece).wait_recv()
            else:
                corner(s, 0).wait_recv()
            relay(s, piece).start()

    def early(s):
        for core in range(2):
            @pl.when(k == core)
            def _(core=core):
                hand_over(s, core)

                @pl.when(turn[core])
                def _():
                    corner(s, core).start()

    def other_corner(s):
        for core in range(2):
            @pl.when(k == core)
            def _(core=core):
                hand_over(s, 1 - core)

    def landed(s, pieces):
        for piece in pieces:
            @pl.when(takes[piece])
            def _(piece=piece):
                relay(s, piece).wait_recv()

    start(0)
    start(1, k)
    probe_copy = remote(probes.at[0], prb.at[k], psem.at[0], psem.at[1], partner)
    probe_copy.start()
    for one in (2, 5, 6):
        local[one].wait()
    for there, at in (
        (has_right, (slice(0, T), far)),
        (has_below, (far, slice(0, T))),
        (has_right & has_below, (far, far)),
    ):
        @pl.when(jnp.logical_not(there))
        def _(at=at):
            for ext in exts:
                for c in range(2):
                    ext[(c,) + at] = jnp.zeros_like(ext[(c,) + at])

    oy, ox = off_ref[0, 0, k, 0], off_ref[0, 0, k, 1]

    def pick(shape_of, axis, low, wrap=False):
        here = lax.broadcasted_iota(jnp.int32, shape_of, axis)
        there = lax.broadcasted_iota(jnp.int32, shape_of, 1 - axis) + low
        if wrap:
            there = there & (E - 1)
        return jnp.where(here == there, 1.0, 0.0).astype(bf16)

    low = slice(0, T)
    row_low, row_far = pick((E, T), 1, oy), pick((E, E), 1, oy - T)
    col_low, col_far = pick((T, E), 0, ox), pick((E, E), 0, ox - T)

    def part(s, by_row, by_col, at):
        result = []
        for c in range(2):
            strip = jnp.dot(by_row, exts[s][(c,) + at], preferred_element_type=f32)
            result.append(jnp.dot(strip.astype(bf16), by_col, preferred_element_type=f32))
        return tuple(result)

    def plus(x, y):
        return (x[0] + y[0], x[1] + y[1])

    def window(s):
        for piece in (2, 3):
            hand_over(s, piece)
        landed(s, (0, 1, 2, 3))
        sides = plus(
            part(s, row_low, col_far, (low, far)), part(s, row_far, col_low, (far, low))
        )
        sides = plus(owns[s], sides)
        hand_over(s, 4)
        landed(s, (4,))
        return plus(sides, part(s, row_far, col_far, (far, far)))

    def transform(v, forward):
        lhs, rhs = (tab.at[0], tab.at[1]) if forward else (tab.at[1], tab.at[0])
        stacked = jnp.concatenate([v[0].astype(bf16), v[1].astype(bf16)], axis=0)
        mid = jnp.dot(lhs[...], stacked, preferred_element_type=f32).astype(bf16)
        wide = jnp.concatenate([mid[0:E], mid[E:]], axis=1)
        result = jnp.dot(wide, rhs[...], preferred_element_type=f32)
        return (result[:, 0:E], result[:, E:])

    modes = range(2)
    owns = []
    for s in range(2):
        local[s].wait()
        owns.append(part(s, row_low, col_low, (low, low)))
    early(0)
    start(1, 1 - k)
    other_corner(0)
    probe_copy.wait()

    def probe(m):
        return (prb[m, 0].astype(f32), prb[m, 1].astype(f32))

    def chirp():
        return (chp[0], chp[1])

    first = window(0)
    props = []
    for m in modes:
        spec = transform(cmul(probe(m), first), True)
        props.append(transform(cmul(chirp(), spec), False))
        if m == 0:
            early(1)
            other_corner(1)
    second = window(1)
    fars = [transform(cmul(props[m], second), True) for m in modes]
    local[3].wait()
    local[4].wait()
    intensity = sum(f[0] * f[0] + f[1] * f[1] for f in fars)
    residual = 2.0 * wts[...] * (intensity - inten[...].astype(f32))
    backs = [transform((residual * fars[m][0], residual * fars[m][1]), False) for m in modes]

    alive = jnp.zeros((E, E), jnp.int32) + k < cnt_ref[0, 0]
    turn_y, turn_x = pick((E, E), 0, oy, True), pick((E, E), 1, ox, True)

    def give(c):
        return remote(gsend.at[other, c], gpart.at[c], gsem.at[c], gsem.at[2 + c], partner)

    def finish(s, parts):
        for c in range(2):
            total = jnp.where(alive, parts[0][c] + parts[1][c], 0.0).astype(bf16)
            turned = jnp.dot(turn_y, total, preferred_element_type=f32).astype(bf16)
            gsend[s, c] = jnp.dot(turned, turn_x, preferred_element_type=f32).astype(bf16)

            @pl.when(k == 1 - s)
            def _():
                give(c).start()

    finish(1, [conj_mul(props[m], backs[m]) for m in modes])

    half = E // 2

    def block(c, y, x, h, w):
        y0, x0 = y % E, x % E
        total = None
        for slot, values in (
            (k, gsend[k, c, y0 : y0 + h, x0 : x0 + w].astype(f32)),
            (other, gpart[c, y0 : y0 + h, x0 : x0 + w].astype(f32)),
        ):
            ypos = lax.broadcasted_iota(jnp.int32, (h, w), 0) + y
            xpos = lax.broadcasted_iota(jnp.int32, (h, w), 1) + x
            low_y, low_x = off_ref[0, 0, slot, 0], off_ref[0, 0, slot, 1]
            inside = (
                (ypos >= low_y) & (ypos < low_y + E) & (xpos >= low_x) & (xpos < low_x + E)
            )
            term = jnp.where(inside, values, 0.0)
            total = term if total is None else total + term
        return total

    def spans(start, stop):
        result = []
        while start < stop:
            end = min(stop, (start // half + 1) * half)
            result.append((start, end - start))
            start = end
        return result

    inner, outer = spans(0, T), spans(T, T + E)

    def fill(dst, c, ys, xs, y_base, x_base, dtype):
        for y, h in ys:
            for x, w in xs:
                dst[y - y_base : y - y_base + h, x - x_base : x - x_base + w] = block(
                    c, y, x, h, w
                ).astype(dtype)

    def push(i):
        src, dst, who = (
            (hd.at[0], rd.at[0], down), (hd.at[1], rd.at[1], right),
            (hb.at[0], rb.at[0], down), (hr.at[1], rr.at[1], right),
            (hb.at[1], rb.at[1], down), (hr.at[0], rr.at[0], right),
        )[i]
        return remote(src, dst, hsend.at[i], hrecv.at[i], who)

    both_out = has_right & has_below
    send_out = (both_out, both_out, has_below, has_right, has_below, has_right)

    def deliver_first():
        for c in range(2):
            give(c).wait_recv()

            @pl.when(both_out)
            def _():
                fill(hd.at[c], c, outer, outer, T, T, bf16)
                push(c).start()

        @pl.when(has_below)
        def _():
            fill(hb.at[0], 0, outer, inner, T, 0, bf16)
            push(2).start()

        @pl.when(has_right)
        def _():
            fill(hr.at[1], 1, inner, outer, 0, T, bf16)
            push(3).start()

    def deliver_second():
        @pl.when(has_below)
        def _():
            fill(hb.at[1], 1, outer, inner, T, 0, bf16)

            @pl.when(has_left)
            def _():
                push(1).wait_recv()
                hb[1, :, 0:E] = (hb[1, :, 0:E].astype(f32) + rd[1].astype(f32)).astype(bf16)

            push(4).start()

        @pl.when(has_right)
        def _():
            fill(hr.at[0], 0, inner, outer, 0, T, bf16)

            @pl.when(has_above)
            def _():
                push(0).wait_recv()
                hr[0, 0:E, :] = (hr[0, 0:E, :].astype(f32) + rd[0].astype(f32)).astype(bf16)

            push(5).start()

    gspecs = [transform(conj_mul(second, backs[m]), True) for m in modes]

    @pl.when(k == 1)
    def _():
        deliver_first()

    finish(0, [
        conj_mul(probe(m), transform(conj_mul(chirp(), gspecs[m]), False)) for m in modes
    ])

    @pl.when(k == 0)
    def _():
        deliver_first()

    deliver_second()
    for c in range(2):
        fill(out_ref.at[0, c], c, inner, inner, 0, 0, f32)

    for i, c, there, land, area in (
        (2, 0, has_above, rb, (near, slice(0, T))),
        (3, 1, has_left, rr, (slice(0, T), near)),
        (4, 1, has_above, rb, (near, slice(0, T))),
        (5, 0, has_left, rr, (slice(0, T), near)),
    ):
        @pl.when(there)
        def _(i=i, c=c, land=land, area=area):
            push(i).wait_recv()
            at = (0, c) + area
            out_ref[at] = out_ref[at] + land[c].astype(f32)

    for s in range(2):
        for piece in range(4):
            @pl.when(sends[piece])
            def _(s=s, piece=piece):
                halo(s, piece).wait_send()
        for piece in range(5):
            @pl.when(takes[piece])
            def _(s=s, piece=piece):
                relay(s, piece).wait_send()
        for core in range(2):
            @pl.when((k == core) & turn[core])
            def _(s=s, core=core):
                corner(s, core).wait_send()
    for c in range(2):
        give(c).wait_send()
    for i in range(6):
        @pl.when(send_out[i])
        def _(i=i):
            push(i).wait_send()


def solution(mesh):
    rows_n, cols_n = mesh.shape["row"], mesh.shape["col"]

    def body(objects, probes, weights, counts, offsets, intensities):
        T, E = objects.shape[2], probes.shape[2]
        W = T + E
        any_space = pl.BlockSpec(memory_space=pl.ANY)
        smem = pl.BlockSpec(memory_space=pltpu.SMEM)
        dma = pltpu.SemaphoreType.DMA
        return pl.pallas_call(
            functools.partial(kernel, (rows_n, cols_n, T, E)),
            out_shape=jax.ShapeDtypeStruct((1, 2, T, T), f32),
            in_specs=[smem, smem] + [any_space] * 6,
            out_specs=pl.BlockSpec(memory_space=pltpu.VMEM),
            scratch_shapes=[
                pltpu.VMEM((2, W, W), bf16), pltpu.VMEM((2, W, W), bf16),
                pltpu.VMEM((2, 2, E, E), bf16), pltpu.VMEM((E, E), f32),
                pltpu.VMEM((E, E), bf16), pltpu.VMEM((2, 2 * E, 2 * E), bf16),
                pltpu.VMEM((2, E, E), f32),
                pltpu.VMEM((2, 2, E, E), bf16),
                pltpu.VMEM((2, E, E), bf16),
                pltpu.VMEM((2, E, T), bf16), pltpu.VMEM((2, T, E), bf16), pltpu.VMEM((2, E, E), bf16),
                pltpu.VMEM((2, E, T), bf16), pltpu.VMEM((2, T, E), bf16), pltpu.VMEM((2, E, E), bf16),
                dma((7,)), dma((2, 5)), dma((2, 5)), dma((2, 5)), dma((2, 5)),
                dma((2,)), dma((4,)), dma((6,)), dma((6,)),
            ],
            compiler_params=pltpu.CompilerParams(
                collective_id=0, has_side_effects=True, vmem_limit_bytes=63 * 1024 * 1024
            ),
            name="ptycho",
        )(
            offsets, counts, objects, probes, weights, intensities,
            jnp.asarray(dft_tables(E)), jnp.asarray(chirp_factor(E)),
        )

    in_specs = (
        P(None, None, ("grp", "row"), "col"),
        P(("grp", "slc"), None, None, None),
        P(),
        P(("grp", "row"), "col"),
        P(("grp", "row"), "col", None, None),
        P(("grp", "row"), "col", None, None, None),
    )
    out_specs = P("slc", None, ("grp", "row"), "col")
    return jax.shard_map(body, mesh=mesh, in_specs=in_specs, out_specs=out_specs, check_vma=False)
```
